32 devices in a mesh: index: 8 (over y, x, core), query: 4 (over z).
Axes of the slice: x: 2, y: 2, z: 4, core: 2. Of those that a mesh axis runs over, the one named last changes fastest.
Arguments:
- queries: bfloat16 [256, 2048], P(('index', 'query')), may hold values from -4 to 4
- slab: bfloat16 [131072, 2048], P(('index', 'query')), may hold values from -24 to 24
- cand_owner: int32 [256, 32], P(('index', 'query')), may hold values from 0 to 31, all different within a row; in each aligned block of 8 rows (0 to 7, 8 to 15, ...) at most 8 rows name the same one
- cand_row: int32 [256, 32], P(('index', 'query')), may hold values from 0 to 4095
Outputs:
- pooled: float32 [256, 256], P(('index', 'query'))
- coarse_lse: float32 [256], P(('index', 'query'))
- margin: float32 [256, 32], P(('index', 'query'))
The draws below stay inside these ranges and needn't reach their ends.
Inputs may be any that keep to these rules, and one draw needn't show every extreme that they name: `cand_owner`: each query names 32 distinct owners. Over the 8 queries of one device (aligned blocks of 8 rows) no owner is named more than 8 times, a bound that some block reaches.
All inputs are finite; a program needn't handle non-finite values.
Results may differ from the reference program's by a relative error of at most 0.00165.
Values may be sent and summed in bfloat16 or wider, within the bound.
No kernel may reach another device: no remote copies, remote signals or barrier semaphores. Data moves between devices by JAX's collectives and lax.ppermute only.
A program may use at most 128 MiB of HBM per device.

```python
import math
import jax
import jax.numpy as jnp
import numpy as np
from jax import lax

W = 2048
PREFIX = 256
K = 32
R_DEV = 4096
QD = 8
Q = 256
ROWS = 131072
CAP = 8
DEVICES = 32


def draw_queries(key, part):
    base = jax.random.normal(jax.random.fold_in(key, 1), (Q, W), jnp.float32)
    return jnp.clip(base, -4.0, 4.0).astype(jnp.bfloat16)


def draw_slab(key, part):
    noise = jnp.clip(jax.random.normal(jax.random.fold_in(key, 2), (ROWS, W), jnp.float32), -4.0, 4.0)
    ramp = 0.75 + 0.5 * jnp.arange(ROWS, dtype=jnp.float32) / ROWS
    row_scale = jnp.exp(jax.random.uniform(jax.random.fold_in(key, 3), (ROWS, 1), jnp.float32, math.log(0.4), math.log(3.0))) * ramp[:, None]
    col_scale = jnp.exp(jax.random.uniform(jax.random.fold_in(key, 4), (1, W), jnp.float32, math.log(0.6), math.log(1.6)))
    values = noise * row_scale * col_scale
    return values.astype(jnp.bfloat16)


def set_ends(result, rng, smallest, largest):
    longest = result.shape.index(max(result.shape))
    spots = []
    for shift in (0, 1):
        where = [jax.random.randint(jax.random.fold_in(rng, axis), (), 0, length) for axis, length in enumerate(result.shape)]
        where[longest] = (where[longest] + shift) % result.shape[longest]
        spots.append(tuple(where))
    return result.at[spots[0]].set(smallest).at[spots[1]].set(largest)


def shared_out(own_key, own, number, rows, count, top, reach, skew):
    order = jax.random.permutation(own_key, count)
    packed, common = load_shares(count, rows * top, reach, skew, True), load_shares(count, rows * top, reach, skew, False)
    places = jnp.arange(count)

    def named(tallies, turn):
        used = int((tallies > 0).sum())
        fixed = max(1, used // 4)
        shifted = fixed + (places - fixed + turn * (used - fixed)) % max(1, count - fixed)
        return jnp.zeros((count,), jnp.int32).at[order[jnp.where(places < fixed, places, shifted)]].set(jnp.asarray(tallies, jnp.int32))

    tallies = jnp.where(number % 4 == 0, named(packed, number // 4), named(common, number - number // 4 - 1))
    mixed = jax.random.permutation(jax.random.fold_in(own, 3), count)
    donor, sink = mixed[0:count // 2 * 2:2], mixed[1:count // 2 * 2:2]
    slack = jnp.minimum(tallies[donor] - 1, reach - tallies[sink]) // 2
    slack = jnp.where((donor == order[0]) | (sink == order[0]) | (tallies[sink] == 0), 0, jnp.maximum(slack, 0))
    shifted = jax.random.randint(jax.random.fold_in(own, 4), (count // 2,), 0, 1 << 20) % (slack + 1)
    tallies = tallies.at[donor].add(-shifted).at[sink].add(shifted)
    members = jnp.searchsorted(jnp.cumsum(tallies), jnp.arange(rows * top), side="right").astype(jnp.int32)
    grid = members.reshape(top, rows).T
    grid = grid[jax.random.permutation(jax.random.fold_in(own, 1), rows)]
    turn = jax.random.randint(jax.random.fold_in(own, 2), (rows, 1), 0, top)
    return jnp.take_along_axis(grid, (jnp.arange(top)[None, :] + turn) % top, axis=1)


def load_shares(amount, total, reach, skew, full):
    portions = [(1 << 20) // math.isqrt(standing ** skew) + 1 for standing in range(1, amount + 1)]
    largest = reach if full else min(reach, max(-(-total // amount), total * portions[0] // sum(portions)))
    least = 1 if total - largest >= amount - 1 else 0
    given, surplus = [largest] + [least] * (amount - 1), total - largest - least * (amount - 1)
    while surplus > 0:
        movable = [i for i in range(1, amount) if given[i] < largest] or [i for i in range(1, amount) if given[i] < reach]
        pool, left = sum([portions[i] for i in movable]), surplus
        for i in movable:
            more = min(reach - given[i], max(1, left * portions[i] // pool), surplus)
            given[i] = given[i] + more
            surplus = surplus - more
    return np.array(given)


def setup_inputs(seed: int = 0) -> dict:
    keys = jax.random.split(jax.random.key(seed), 5)
    queries = draw_queries(jax.random.fold_in(keys[4], 71), 0)
    slab = draw_slab(jax.random.fold_in(keys[4], 71), 0)
    cand_owner_keys = jax.random.split(jax.random.fold_in(keys[2], 1), Q // QD)
    cand_owner_turns = jax.random.permutation(jax.random.fold_in(keys[2], 3), Q // QD)
    cand_owner = jax.vmap(lambda own, number: shared_out(jax.random.fold_in(keys[2], 2), own, number, QD, DEVICES, K, CAP, 2))(cand_owner_keys, cand_owner_turns).reshape((Q, K))
    cand_row = set_ends(jax.random.randint(keys[3], (Q, K), 0, R_DEV), jax.random.fold_in(keys[3], 1), 0, R_DEV - 1).astype(jnp.int32)
    return {"queries": queries, "slab": slab, "cand_owner": cand_owner, "cand_row": cand_row}


def reference(queries, slab, cand_owner, cand_row):
    prefix_keys = slab[:, :PREFIX]
    blk = min(Q, 256)
    nblk = Q // blk
    scale = PREFIX ** -0.5

    def coarse(query_block):
        logits = lax.dot_general(query_block, prefix_keys, (((1,), (1,)), ((), ())), preferred_element_type=jnp.float32) * scale
        top = jnp.max(logits, axis=1)
        weights = jnp.exp(logits - top[:, None])
        total = jnp.sum(weights, axis=1)
        pooled_sum = jnp.dot(weights.astype(jnp.bfloat16), prefix_keys, preferred_element_type=jnp.float32)
        return pooled_sum / total[:, None], top + jnp.log(total)

    pooled, lse = lax.map(coarse, queries[:, :PREFIX].reshape(nblk, blk, PREFIX))
    pooled = pooled.reshape(Q, PREFIX)
    lse = lse.reshape(Q)
    cand = (cand_owner * R_DEV + cand_row).astype(jnp.int32)

    def fine(pair):
        query_block, id_block = pair
        rows = slab[id_block]
        return jnp.einsum("qw,qkw->qk", query_block.astype(jnp.float32), rows.astype(jnp.float32))

    full = lax.map(fine, (queries.reshape(nblk, blk, W), cand.reshape(nblk, blk, K)))
    full = full.reshape(Q, K) * (W ** -0.5)
    margin = full - lse[:, None]
    return pooled, lse, margin
```

```python
import functools
import jax
import jax.numpy as jnp
from jax import lax
from jax.experimental import pallas as pl
from jax.experimental.pallas import tpu as pltpu
from jax.sharding import PartitionSpec as P

PREFIX = 256
AXES = ("index", "query")
RADIX = 64


def xor_stages(index_size, query_size):
    q_bits = query_size.bit_length() - 1
    i_bits = index_size.bit_length() - 1
    bits = [list(range(q_bits)), list(range(q_bits + 1, q_bits + i_bits)), [q_bits]]
    stages = []
    for group in bits:
        for at in range(0, len(group), 2):
            pair = group[at : at + 2]
            offs = [1 << pair[0]]
            if len(pair) == 2:
                offs += [1 << pair[1], (1 << pair[0]) | (1 << pair[1])]
            stages.append(offs)
    return stages


def swap(x, off, devices):
    return lax.ppermute(x, AXES, [(d, d ^ off) for d in range(devices)])


def pack_body(q_ref, owner_ref, row_ref, out_ref, *, width, lanes, owners):
    out_ref[:, :width] = q_ref[...]
    lane = lax.broadcasted_iota(jnp.int32, (q_ref.shape[0], lanes), 1)
    table = jnp.zeros(lane.shape, jnp.int32)
    for k in range(owner_ref.shape[1]):
        own = owner_ref[:, k : k + 1]
        row = row_ref[:, k : k + 1] + 1
        table += jnp.where(lane == own, row // RADIX, 0)
        table += jnp.where(lane == own + owners, row % RADIX, 0)
    out_ref[:, width:] = table.astype(jnp.float32).astype(jnp.bfloat16)


def score_body(me_ref, g_ref, slab_ref, out_ref, rows_ref, logit_ref, sems, *, width, owners, chunk):
    r_dev = slab_ref.shape[0]
    n_q = g_ref.shape[0]
    n_chunks = r_dev // chunk
    scale = PREFIX ** (-0.5)

    def copy(c):
        at = pl.ds(c * chunk, chunk)
        return pltpu.make_async_copy(slab_ref.at[at], rows_ref.at[at], sems.at[c])

    @pl.when(pl.program_id(0) == 0)
    def _():
        for c in range(n_chunks):
            copy(c).start()

    me = me_ref[0]
    tab = g_ref[:, width:].astype(jnp.float32)
    lane = lax.broadcasted_iota(jnp.int32, tab.shape, 1)
    weight = jnp.where(lane == me, float(RADIX), 0.0) + jnp.where(lane == me + owners, 1.0, 0.0)
    want = jnp.sum(tab * weight, axis=1, keepdims=True).astype(jnp.int32) - 1

    best = jnp.full((n_q, 128), -jnp.inf, jnp.float32)
    score = jnp.zeros((n_q, 128), jnp.float32)
    contract = (((1,), (1,)), ((), ()))
    for c in range(n_chunks):
        at = slice(c * chunk, (c + 1) * chunk)

        @pl.when(pl.program_id(0) == 0)
        def _():
            copy(c).wait()

        logits = lax.dot_general(
            g_ref[:, :PREFIX], rows_ref[at, :PREFIX], contract, preferred_element_type=jnp.float32
        )
        logit_ref[:, at] = logits
        full = lax.dot_general(
            g_ref[:, PREFIX:width], rows_ref[at, PREFIX:], contract, preferred_element_type=jnp.float32
        )
        full = full + logits
        col = lax.broadcasted_iota(jnp.int32, (n_q, 128), 1)
        for s in range(chunk // 128):
            part = slice(s * 128, (s + 1) * 128)
            best = jnp.maximum(best, logits[:, part])
            score += jnp.where(col + (c * chunk + s * 128) == want, full[:, part], 0.0)
    top = jnp.max(best, axis=1, keepdims=True)
    score = jnp.sum(score, axis=1, keepdims=True) * width ** (-0.5)
    acc = jnp.zeros((n_q, PREFIX), jnp.float32)
    total = jnp.zeros((n_q, 128), jnp.float32)
    for c in range(n_chunks):
        at = slice(c * chunk, (c + 1) * chunk)
        weights = jnp.exp((logit_ref[:, at] - top) * scale)
        for s in range(chunk // 128):
            total += weights[:, s * 128 : (s + 1) * 128]
        acc += jnp.dot(
            weights.astype(jnp.bfloat16), rows_ref[at, :PREFIX], preferred_element_type=jnp.float32
        )
    total = jnp.sum(total, axis=1, keepdims=True)
    tail = out_ref.shape[1] - PREFIX
    lane = lax.broadcasted_iota(jnp.int32, (n_q, tail), 1)
    out_ref[:, :PREFIX] = acc
    out_ref[:, PREFIX:] = jnp.where(
        lane == tail - 1, top * scale, jnp.where(lane == tail - 2, total, jnp.where(lane == me, score, 0.0))
    )


def merge(parts):
    wide = parts[0].shape[1]
    tops = [p[:, wide - 1 :] for p in parts]
    top = functools.reduce(jnp.maximum, tops)
    lane = lax.broadcasted_iota(jnp.int32, parts[0].shape, 1)
    scaled = (lane < PREFIX) | (lane == wide - 2)
    out = jnp.zeros(parts[0].shape, jnp.float32)
    for part, t in zip(parts, tops):
        out += part * jnp.where(scaled, jnp.exp(t - top), 1.0)
    return jnp.where(lane == wide - 1, top, out)


def merge_body(*refs):
    refs[-1][...] = merge([r[...] for r in refs[:-1]])


def finish_body(owner_ref, *refs, owners):
    parts, (pooled_ref, lse_ref, margin_ref) = refs[:-3], refs[-3:]
    out = merge([r[...] for r in parts])
    wide = out.shape[1]
    total = out[:, wide - 2 : wide - 1]
    lse = out[:, wide - 1 :] + jnp.log(total)
    pooled_ref[...] = out[:, :PREFIX] / total
    lse_ref[...] = lse
    own = owner_ref[...]
    full = jnp.zeros(own.shape, jnp.float32)
    for o in range(owners):
        full += jnp.where(own == o, out[:, PREFIX + o : PREFIX + o + 1], 0.0)
    margin_ref[...] = full - lse


def on_device(queries, slab, cand_owner, cand_row, *, index_size, query_size):
    devices = index_size * query_size
    q_dev, width = queries.shape
    owners = devices
    stages = xor_stages(index_size, query_size)
    lanes = -(-2 * owners // 128) * 128
    tail = -(-(owners + 2) // 128) * 128
    me = lax.axis_index(AXES).astype(jnp.int32).reshape(1)
    f32 = jnp.float32

    x = pl.pallas_call(
        functools.partial(pack_body, width=width, lanes=lanes, owners=owners),
        out_shape=jax.ShapeDtypeStruct((q_dev, width + lanes), jnp.bfloat16),
        name="pack",
    )(queries, cand_owner, cand_row)
    for offs in stages:
        x = jnp.concatenate([x] + [swap(x, off, devices) for off in offs], axis=0)

    n_q = x.shape[0]
    block = min(n_q, 256)
    r_dev = slab.shape[0]
    chunk = 512
    out = pl.pallas_call(
        functools.partial(score_body, width=width, owners=owners, chunk=chunk),
        grid=(n_q // block,),
        in_specs=[
            pl.BlockSpec(memory_space=pltpu.SMEM),
            pl.BlockSpec((block, width + lanes), lambda i: (i, 0)),
            pl.BlockSpec(memory_space=pl.ANY),
        ],
        out_specs=pl.BlockSpec((block, PREFIX + tail), lambda i: (i, 0)),
        out_shape=jax.ShapeDtypeStruct((n_q, PREFIX + tail), f32),
        scratch_shapes=[
            pltpu.VMEM((r_dev, width), jnp.bfloat16),
            pltpu.VMEM((block, r_dev), f32),
            pltpu.SemaphoreType.DMA((r_dev // chunk,)),
        ],
        compiler_params=pltpu.CompilerParams(vmem_limit_bytes=60000 * 1024),
        name="score",
    )(me, x, slab)

    for number, offs in enumerate(reversed(stages)):
        n = out.shape[0] // (len(offs) + 1)
        mine = [out[:n]] + [
            swap(out[(j + 1) * n : (j + 2) * n], off, devices) for j, off in enumerate(offs)
        ]
        if number < len(stages) - 1:
            out = pl.pallas_call(
                merge_body, out_shape=jax.ShapeDtypeStruct((n, PREFIX + tail), f32), name="merge"
            )(*mine)
    pooled, lse, margin = pl.pallas_call(
        functools.partial(finish_body, owners=owners),
        out_shape=(
            jax.ShapeDtypeStruct((q_dev, PREFIX), f32),
            jax.ShapeDtypeStruct((q_dev, 1), f32),
            jax.ShapeDtypeStruct(cand_owner.shape, f32),
        ),
        name="finish",
    )(cand_owner, *mine)
    return pooled, lse.reshape(q_dev), margin


def solution(mesh):
    spec = P(AXES, None)
    body = functools.partial(
        on_device, index_size=mesh.shape["index"], query_size=mesh.shape["query"]
    )
    return jax.shard_map(
        body,
        mesh=mesh,
        in_specs=(spec, spec, spec, spec),
        out_specs=(spec, P(AXES), spec),
        check_vma=False,
    )
```

```python
import functools
import jax
import jax.numpy as jnp
from jax import lax
from jax.experimental import pallas as pl
from jax.experimental.pallas import tpu as pltpu
from jax.sharding import PartitionSpec as P

PREFIX = 256
AXES = ("index", "query")
RADIX = 64


def xor_stages(index_size, query_size):
    q_bits = query_size.bit_length() - 1
    i_bits = index_size.bit_length() - 1
    bits = [list(range(q_bits)), list(range(q_bits + 1, q_bits + i_bits)), [q_bits]]
    stages = []
    for group in bits:
        for at in range(0, len(group), 2):
            pair = group[at : at + 2]
            offs = [1 << pair[0]]
            if len(pair) == 2:
                offs += [1 << pair[1], (1 << pair[0]) | (1 << pair[1])]
            stages.append(offs)
    return stages


def swap(x, off, devices):
    return lax.ppermute(x, AXES, [(d, d ^ off) for d in range(devices)])


SMALL = pltpu.CompilerParams(vmem_limit_bytes=16 << 20)


def in_vmem(*arrays):
    return [pltpu.with_memory_space_constraint(a, pltpu.VMEM) for a in arrays]


def join_body(*refs):
    out_ref = refs[-1]
    at = 0
    for ref in refs[:-1]:
        out_ref[at : at + ref.shape[0], :] = ref[...]
        at += ref.shape[0]


def join(parts):
    rows = sum(p.shape[0] for p in parts)
    return pl.pallas_call(
        join_body, out_shape=pltpu.VMEM((rows, parts[0].shape[1]), parts[0].dtype), compiler_params=SMALL, name="join"
    )(*in_vmem(*parts))


def pack_body(q_ref, owner_ref, row_ref, out_ref, *, width, lanes, owners):
    out_ref[:, :width] = q_ref[...]
    lane = lax.broadcasted_iota(jnp.int32, (q_ref.shape[0], lanes), 1)
    table = jnp.zeros(lane.shape, jnp.int32)
    for k in range(owner_ref.shape[1]):
        own = owner_ref[:, k : k + 1]
        row = row_ref[:, k : k + 1] + 1
        table += jnp.where(lane == own, row // RADIX, 0)
        table += jnp.where(lane == own + owners, row % RADIX, 0)
    out_ref[:, width:] = table.astype(jnp.float32).astype(jnp.bfloat16)


def score_body(me_ref, x_ref, y_ref, slab_ref, keep_ref, send_ref, g_ref, rows_ref, logit_ref, sems, *, width, owners, chunk):
    r_dev = slab_ref.shape[0]
    n_q = g_ref.shape[0]
    half = n_q // 2
    g_ref[:half, :] = x_ref[...]
    g_ref[half:, :] = y_ref[...]
    n_chunks = r_dev // chunk
    scale = PREFIX ** (-0.5)

    def copy(c):
        at = pl.ds(c * chunk, chunk)
        return pltpu.make_async_copy(slab_ref.at[at], rows_ref.at[at], sems.at[c])

    @pl.when(pl.program_id(0) == 0)
    def _():
        for c in range(n_chunks):
            copy(c).start()

    me = me_ref[0]
    tab = g_ref[:, width:].astype(jnp.float32)
    lane = lax.broadcasted_iota(jnp.int32, tab.shape, 1)
    weight = jnp.where(lane == me, float(RADIX), 0.0) + jnp.where(lane == me + owners, 1.0, 0.0)
    want = jnp.sum(tab * weight, axis=1, keepdims=True).astype(jnp.int32) - 1

    best = jnp.full((n_q, 128), -jnp.inf, jnp.float32)
    score = jnp.zeros((n_q, 128), jnp.float32)
    contract = (((1,), (1,)), ((), ()))
    for c in range(n_chunks):
        at = slice(c * chunk, (c + 1) * chunk)

        @pl.when(pl.program_id(0) == 0)
        def _():
            copy(c).wait()

        logits = lax.dot_general(
            g_ref[:, :PREFIX], rows_ref[at, :PREFIX], contract, preferred_element_type=jnp.float32
        )
        logit_ref[:, at] = logits
        full = lax.dot_general(
            g_ref[:, PREFIX:width], rows_ref[at, PREFIX:], contract, preferred_element_type=jnp.float32
        )
        full = full + logits
        col = lax.broadcasted_iota(jnp.int32, (n_q, 128), 1)
        for s in range(chunk // 128):
            part = slice(s * 128, (s + 1) * 128)
            best = jnp.maximum(best, logits[:, part])
            score += jnp.where(col + (c * chunk + s * 128) == want, full[:, part], 0.0)
    top = jnp.max(best, axis=1, keepdims=True)
    score = jnp.sum(score, axis=1, keepdims=True) * width ** (-0.5)
    acc = jnp.zeros((n_q, PREFIX), jnp.float32)
    total = jnp.zeros((n_q, 128), jnp.float32)
    for c in range(n_chunks):
        at = slice(c * chunk, (c + 1) * chunk)
        weights = jnp.exp((logit_ref[:, at] - top) * scale)
        for s in range(chunk // 128):
            total += weights[:, s * 128 : (s + 1) * 128]
        acc += jnp.dot(
            weights.astype(jnp.bfloat16), rows_ref[at, :PREFIX], preferred_element_type=jnp.float32
        )
    total = jnp.sum(total, axis=1, keepdims=True)
    tail = keep_ref.shape[1] - PREFIX
    lane = lax.broadcasted_iota(jnp.int32, (n_q, tail), 1)
    rest = jnp.where(
        lane == tail - 1, top * scale, jnp.where(lane == tail - 2, total, jnp.where(lane == me, score, 0.0))
    )
    keep_ref[:, :PREFIX] = acc[:half, :]
    keep_ref[:, PREFIX:] = rest[:half, :]
    send_ref[:, :PREFIX] = acc[half:, :]
    send_ref[:, PREFIX:] = rest[half:, :]


def merge(parts):
    wide = parts[0].shape[1]
    tops = [p[:, wide - 1 :] for p in parts]
    top = functools.reduce(jnp.maximum, tops)
    lane = lax.broadcasted_iota(jnp.int32, parts[0].shape, 1)
    scaled = (lane < PREFIX) | (lane == wide - 2)
    out = jnp.zeros(parts[0].shape, jnp.float32)
    for part, t in zip(parts, tops):
        out += part * jnp.where(scaled, jnp.exp(t - top), 1.0)
    return jnp.where(lane == wide - 1, top, out)


def merge_body(*refs, n_parts):
    out = merge([r[...] for r in refs[:n_parts]])
    at = 0
    for ref in refs[n_parts:]:
        ref[...] = out[at : at + ref.shape[0], :]
        at += ref.shape[0]


def finish_body(owner_ref, *refs, owners):
    parts, (pooled_ref, lse_ref, margin_ref) = refs[:-3], refs[-3:]
    out = merge([r[...] for r in parts])
    wide = out.shape[1]
    total = out[:, wide - 2 : wide - 1]
    lse = out[:, wide - 1 :] + jnp.log(total)
    pooled_ref[...] = out[:, :PREFIX] / total
    n = lse.shape[0]
    square = (n, n)
    eye = lax.broadcasted_iota(jnp.int32, square, 0) == lax.broadcasted_iota(jnp.int32, square, 1)
    lse_ref[...] = jnp.sum(jnp.where(eye, lse, 0.0), axis=0, keepdims=True)
    own = owner_ref[...]
    full = jnp.zeros(own.shape, jnp.float32)
    for o in range(owners):
        full += jnp.where(own == o, out[:, PREFIX + o : PREFIX + o + 1], 0.0)
    margin_ref[...] = full - lse


def on_device(queries, slab, cand_owner, cand_row, *, index_size, query_size):
    devices = index_size * query_size
    q_dev, width = queries.shape
    owners = devices
    stages = xor_stages(index_size, query_size)
    lanes = -(-2 * owners // 128) * 128
    tail = -(-(owners + 2) // 128) * 128
    me = lax.axis_index(AXES).astype(jnp.int32).reshape(1)
    f32 = jnp.float32

    x = pl.pallas_call(
        functools.partial(pack_body, width=width, lanes=lanes, owners=owners),
        out_shape=pltpu.VMEM((q_dev, width + lanes), jnp.bfloat16),
        compiler_params=SMALL,
        name="pack",
    )(queries, cand_owner, cand_row)
    for offs in stages[:-1]:
        x = join([x] + [swap(x, off, devices) for off in offs])
    y = swap(x, stages[-1][0], devices)

    n_half = x.shape[0]
    half = min(n_half, 128)
    wide = PREFIX + tail
    r_dev = slab.shape[0]
    chunk = 512
    pair = [pl.BlockSpec((half, width + lanes), lambda i: (i, 0))] * 2
    if n_half == half:
        pair = [pl.BlockSpec(memory_space=pltpu.VMEM)] * 2
        x, y = in_vmem(x, y)
        outs = [pl.BlockSpec(memory_space=pltpu.VMEM)] * 2
        shape = pltpu.VMEM((n_half, wide), f32)
    else:
        outs = [pl.BlockSpec((half, wide), lambda i: (i, 0))] * 2
        shape = jax.ShapeDtypeStruct((n_half, wide), f32)
    keep, send = pl.pallas_call(
        functools.partial(score_body, width=width, owners=owners, chunk=chunk),
        grid=(n_half // half,),
        in_specs=[pl.BlockSpec(memory_space=pltpu.SMEM), *pair, pl.BlockSpec(memory_space=pl.ANY)],
        out_specs=outs,
        out_shape=(shape, shape),
        scratch_shapes=[
            pltpu.VMEM((2 * half, width + lanes), jnp.bfloat16),
            pltpu.VMEM((r_dev, width), jnp.bfloat16),
            pltpu.VMEM((2 * half, r_dev), f32),
            pltpu.SemaphoreType.DMA((r_dev // chunk,)),
        ],
        compiler_params=pltpu.CompilerParams(vmem_limit_bytes=36000 * 1024),
        name="score",
    )(me, x, y, slab)

    parts = [keep, swap(send, stages[-1][0], devices)]
    for offs in reversed(stages[:-1]):
        n = parts[0].shape[0] // (len(offs) + 1)
        keep, *sends = pl.pallas_call(
            functools.partial(merge_body, n_parts=len(parts)),
            out_shape=tuple(pltpu.VMEM((n, wide), f32) for _ in range(len(offs) + 1)),
            compiler_params=SMALL,
            name="merge",
        )(*in_vmem(*parts))
        parts = [keep] + [swap(s, off, devices) for s, off in zip(sends, offs)]
    pooled, lse, margin = pl.pallas_call(
        functools.partial(finish_body, owners=owners),
        out_shape=(
            jax.ShapeDtypeStruct((q_dev, PREFIX), f32),
            jax.ShapeDtypeStruct((1, q_dev), f32),
            jax.ShapeDtypeStruct(cand_owner.shape, f32),
        ),
        compiler_params=SMALL,
        name="finish",
    )(cand_owner, *in_vmem(*parts))
    return pooled, lse.reshape(q_dev), margin


def solution(mesh):
    spec = P(AXES, None)
    body = functools.partial(
        on_device, index_size=mesh.shape["index"], query_size=mesh.shape["query"]
    )
    return jax.shard_map(
        body,
        mesh=mesh,
        in_specs=(spec, spec, spec, spec),
        out_specs=(spec, P(AXES), spec),
        check_vma=False,
    )
```

```python
import functools
import jax
import jax.numpy as jnp
from jax import lax
from jax.experimental import pallas as pl
from jax.experimental.pallas import tpu as pltpu
from jax.sharding import PartitionSpec as P


PREFIX = 256
AXES = ("index", "query")
RADIX = 64


def xor_stages(index_size, query_size):
    q_bits = query_size.bit_length() - 1
    i_bits = index_size.bit_length() - 1
    bits = [list(range(q_bits)), list(range(q_bits + 1, q_bits + i_bits)), [q_bits]]
    stages = []
    for group in bits:
        for at in range(0, len(group), 2):
            pair = group[at : at + 2]
            offs = [1 << pair[0]]
            if len(pair) == 2:
                offs += [1 << pair[1], (1 << pair[0]) | (1 << pair[1])]
            stages.append(offs)
    return stages


def swap(x, off, devices):
    return lax.ppermute(x, AXES, [(d, d ^ off) for d in range(devices)])


SMALL = pltpu.CompilerParams(vmem_limit_bytes=16 << 20)


def in_vmem(*arrays):
    return [pltpu.with_memory_space_constraint(a, pltpu.VMEM) for a in arrays]


def in_hbm(*arrays):
    return [pltpu.with_memory_space_constraint(a, pltpu.HBM) for a in arrays]


def join_body(*refs):
    out_ref = refs[-1]
    at = 0
    for ref in refs[:-1]:
        out_ref[at : at + ref.shape[0], :] = ref[...]
        at += ref.shape[0]


def join(parts):
    rows = sum(p.shape[0] for p in parts)
    return pl.pallas_call(
        join_body, out_shape=pltpu.VMEM((rows, parts[0].shape[1]), parts[0].dtype), compiler_params=SMALL, name="join"
    )(*in_vmem(*parts))


def load_body(from_ref, out_ref, sem, *, first):
    rows = out_ref.shape[0]
    copy = pltpu.make_async_copy(from_ref.at[pl.ds(first, rows)], out_ref, sem)
    copy.start()
    copy.wait()


def load(slab, first, rows):
    return pl.pallas_call(
        functools.partial(load_body, first=first),
        in_specs=[pl.BlockSpec(memory_space=pltpu.HBM)],
        out_shape=pltpu.VMEM((rows, slab.shape[1]), slab.dtype),
        scratch_shapes=[pltpu.SemaphoreType.DMA],
        compiler_params=SMALL,
        cost_estimate=pl.CostEstimate(
            flops=0, transcendentals=0, bytes_accessed=2 * rows * slab.shape[1]
        ),
        name="load",
    )(*in_hbm(slab))


def pack_body(q_hbm, owner_hbm, row_hbm, out_ref, owner_ref, row_ref, sems, *, width, lanes, owners):
    copies = [
        pltpu.make_async_copy(owner_hbm, owner_ref, sems.at[0]),
        pltpu.make_async_copy(row_hbm, row_ref, sems.at[1]),
        pltpu.make_async_copy(q_hbm, out_ref.at[:, pl.ds(0, width)], sems.at[2]),
    ]
    for copy in copies:
        copy.start()
    copies[0].wait()
    copies[1].wait()
    lane = lax.broadcasted_iota(jnp.int32, (owner_ref.shape[0], lanes), 1)
    table = jnp.zeros(lane.shape, jnp.int32)
    for k in range(owner_ref.shape[1]):
        own = owner_ref[:, k : k + 1]
        row = row_ref[:, k : k + 1] + 1
        table += jnp.where(lane == own, row // RADIX, 0)
        table += jnp.where(lane == own + owners, row % RADIX, 0)
    out_ref[:, width:] = table.astype(jnp.float32).astype(jnp.bfloat16)
    copies[2].wait()


def score_body(x_ref, y_ref, rows_a, rows_b, rows_c, keep_ref, send_ref, g_ref, logit_ref, *, width, owners, chunk):
    rows = [
        (ref, slice(at, at + chunk))
        for ref in (rows_a, rows_b, rows_c)
        for at in range(0, ref.shape[0], chunk)
    ]
    n_q = g_ref.shape[0]
    half = n_q // 2
    g_ref[:half, :] = x_ref[...]
    g_ref[half:, :] = y_ref[...]
    n_chunks = len(rows)
    scale = PREFIX ** (-0.5)

    me = lax.axis_index("index") * lax.axis_size("query") + lax.axis_index("query")
    tab = g_ref[:, width:].astype(jnp.float32)
    lane = lax.broadcasted_iota(jnp.int32, tab.shape, 1)
    weight = jnp.where(lane == me, float(RADIX), 0.0) + jnp.where(lane == me + owners, 1.0, 0.0)
    want = jnp.sum(tab * weight, axis=1, keepdims=True).astype(jnp.int32) - 1

    best = jnp.full((n_q, 128), -jnp.inf, jnp.float32)
    score = jnp.zeros((n_q, 128), jnp.float32)
    contract = (((1,), (1,)), ((), ()))
    for c in range(n_chunks):
        at = slice(c * chunk, (c + 1) * chunk)
        ref, own = rows[c]
        logits = lax.dot_general(
            g_ref[:, :PREFIX], ref[own, :PREFIX], contract, preferred_element_type=jnp.float32
        )
        logit_ref[:, at] = logits
        full = lax.dot_general(
            g_ref[:, PREFIX:width], ref[own, PREFIX:], contract, preferred_element_type=jnp.float32
        )
        full = full + logits
        col = lax.broadcasted_iota(jnp.int32, (n_q, 128), 1)
        for s in range(chunk // 128):
            part = slice(s * 128, (s + 1) * 128)
            best = jnp.maximum(best, logits[:, part])
            score += jnp.where(col + (c * chunk + s * 128) == want, full[:, part], 0.0)
    top = jnp.max(best, axis=1, keepdims=True)
    score = jnp.sum(score, axis=1, keepdims=True) * width ** (-0.5)
    acc = jnp.zeros((n_q, PREFIX), jnp.float32)
    total = jnp.zeros((n_q, 128), jnp.float32)
    for c in range(n_chunks):
        at = slice(c * chunk, (c + 1) * chunk)
        ref, own = rows[c]
        weights = jnp.exp((logit_ref[:, at] - top) * scale)
        for s in range(chunk // 128):
            total += weights[:, s * 128 : (s + 1) * 128]
        acc += jnp.dot(
            weights.astype(jnp.bfloat16), ref[own, :PREFIX], preferred_element_type=jnp.float32
        )
    total = jnp.sum(total, axis=1, keepdims=True)
    tail = keep_ref.shape[1] - PREFIX
    lane = lax.broadcasted_iota(jnp.int32, (n_q, tail), 1)
    rest = jnp.where(
        lane == tail - 1, top * scale, jnp.where(lane == tail - 2, total, jnp.where(lane == me, score, 0.0))
    )
    keep_ref[:, :PREFIX] = acc[:half, :]
    keep_ref[:, PREFIX:] = rest[:half, :]
    send_ref[:, :PREFIX] = acc[half:, :]
    send_ref[:, PREFIX:] = rest[half:, :]


def merge(parts):
    wide = parts[0].shape[1]
    tops = [p[:, wide - 1 :] for p in parts]
    top = functools.reduce(jnp.maximum, tops)
    lane = lax.broadcasted_iota(jnp.int32, parts[0].shape, 1)
    scaled = (lane < PREFIX) | (lane == wide - 2)
    out = jnp.zeros(parts[0].shape, jnp.float32)
    for part, t in zip(parts, tops):
        out += part * jnp.where(scaled, jnp.exp(t - top), 1.0)
    return jnp.where(lane == wide - 1, top, out)


def merge_body(*refs, n_parts):
    out = merge([r[...] for r in refs[:n_parts]])
    at = 0
    for ref in refs[n_parts:]:
        ref[...] = out[at : at + ref.shape[0], :]
        at += ref.shape[0]


def finish_body(owner_ref, *refs, owners):
    parts, (pooled_ref, lse_ref, margin_ref) = refs[:-3], refs[-3:]
    out = merge([r[...] for r in parts])
    wide = out.shape[1]
    total = out[:, wide - 2 : wide - 1]
    lse = out[:, wide - 1 :] + jnp.log(total)
    pooled_ref[...] = out[:, :PREFIX] / total
    n = lse.shape[0]
    square = (n, n)
    eye = lax.broadcasted_iota(jnp.int32, square, 0) == lax.broadcasted_iota(jnp.int32, square, 1)
    lse_ref[...] = jnp.sum(jnp.where(eye, lse, 0.0), axis=0, keepdims=True)
    own = owner_ref[...]
    full = jnp.zeros(own.shape, jnp.float32)
    for o in range(owners):
        full += jnp.where(own == o, out[:, PREFIX + o : PREFIX + o + 1], 0.0)
    margin_ref[...] = full - lse


def on_device(queries, slab, cand_owner, cand_row, *, index_size, query_size):
    devices = index_size * query_size
    q_dev, width = queries.shape
    owners = devices
    stages = xor_stages(index_size, query_size)
    lanes = -(-2 * owners // 128) * 128
    tail = -(-(owners + 2) // 128) * 128
    f32 = jnp.float32

    x = pl.pallas_call(
        functools.partial(pack_body, width=width, lanes=lanes, owners=owners),
        in_specs=[pl.BlockSpec(memory_space=pltpu.HBM)] * 3,
        out_shape=pltpu.VMEM((q_dev, width + lanes), jnp.bfloat16),
        scratch_shapes=[
            pltpu.VMEM(cand_owner.shape, jnp.int32),
            pltpu.VMEM(cand_row.shape, jnp.int32),
            pltpu.SemaphoreType.DMA((3,)),
        ],
        compiler_params=SMALL,
        name="pack",
    )(*in_hbm(queries, cand_owner, cand_row))
    r_dev = slab.shape[0]
    chunk = 512
    cuts = [0, 3 * r_dev // 8, 7 * r_dev // 8, r_dev]
    pieces = []
    for offs in stages[:-1]:
        got = [swap(x, off, devices) for off in offs]
        if len(pieces) < 2:
            at = len(pieces)
            pieces.append(load(slab, cuts[at], cuts[at + 1] - cuts[at]))
        x = join([x] + got)
    y = swap(x, stages[-1][0], devices)
    pieces.append(load(slab, cuts[2], cuts[3] - cuts[2]))

    n_half = x.shape[0]
    half = min(n_half, 128)
    wide = PREFIX + tail
    pair = [pl.BlockSpec((half, width + lanes), lambda i: (i, 0))] * 2
    if n_half == half:
        pair = [pl.BlockSpec(memory_space=pltpu.VMEM)] * 2
        x, y = in_vmem(x, y)
        outs = [pl.BlockSpec(memory_space=pltpu.VMEM)] * 2
        shape = pltpu.VMEM((n_half, wide), f32)
    else:
        outs = [pl.BlockSpec((half, wide), lambda i: (i, 0))] * 2
        shape = jax.ShapeDtypeStruct((n_half, wide), f32)
    keep, send = pl.pallas_call(
        functools.partial(score_body, width=width, owners=owners, chunk=chunk),
        grid=(n_half // half,),
        in_specs=[*pair, *[pl.BlockSpec(memory_space=pltpu.VMEM)] * 3],
        out_specs=outs,
        out_shape=(shape, shape),
        scratch_shapes=[
            pltpu.VMEM((2 * half, width + lanes), jnp.bfloat16),
            pltpu.VMEM((2 * half, r_dev), f32),
        ],
        compiler_params=pltpu.CompilerParams(vmem_limit_bytes=20 << 20),
        name="score",
    )(x, y, *in_vmem(*pieces))

    parts = [keep, swap(send, stages[-1][0], devices)]
    for offs in reversed(stages[:-1]):
        n = parts[0].shape[0] // (len(offs) + 1)
        keep, *sends = pl.pallas_call(
            functools.partial(merge_body, n_parts=len(parts)),
            out_shape=tuple(pltpu.VMEM((n, wide), f32) for _ in range(len(offs) + 1)),
            compiler_params=SMALL,
            name="merge",
        )(*in_vmem(*parts))
        parts = [keep] + [swap(s, off, devices) for s, off in zip(sends, offs)]
    pooled, lse, margin = pl.pallas_call(
        functools.partial(finish_body, owners=owners),
        out_shape=(
            jax.ShapeDtypeStruct((q_dev, PREFIX), f32),
            jax.ShapeDtypeStruct((1, q_dev), f32),
            jax.ShapeDtypeStruct(cand_owner.shape, f32),
        ),
        compiler_params=SMALL,
        name="finish",
    )(cand_owner, *in_vmem(*parts))
    return pooled, lse.reshape(q_dev), margin


def solution(mesh):
    spec = P(AXES, None)
    body = functools.partial(
        on_device, index_size=mesh.shape["index"], query_size=mesh.shape["query"]
    )
    return jax.shard_map(
        body,
        mesh=mesh,
        in_specs=(spec, spec, spec, spec),
        out_specs=(spec, P(AXES), spec),
        check_vma=False,
    )
```

```python
import functools
import jax
import jax.numpy as jnp
from jax import lax
from jax.experimental import pallas as pl
from jax.experimental.pallas import tpu as pltpu
from jax.sharding import PartitionSpec as P


PREFIX = 256
AXES = ("index", "query")
RADIX = 64


def xor_stages(index_size, query_size):
    q_bits = query_size.bit_length() - 1
    i_bits = index_size.bit_length() - 1
    bits = [list(range(q_bits)), list(range(q_bits + 1, q_bits + i_bits)), [q_bits]]
    stages = []
    for group in bits:
        for at in range(0, len(group), 2):
            pair = group[at : at + 2]
            offs = [1 << pair[0]]
            if len(pair) == 2:
                offs += [1 << pair[1], (1 << pair[0]) | (1 << pair[1])]
            stages.append(offs)
    return stages


def swap(x, off, devices):
    return lax.ppermute(x, AXES, [(d, d ^ off) for d in range(devices)])


SMALL = pltpu.CompilerParams(vmem_limit_bytes=16 << 20)


def swaps(arrays, offs, devices):
    out = []
    for x, off in zip(arrays, offs):
        out.append(swap(x, off, devices))
    return out


def in_vmem(*arrays):
    return [pltpu.with_memory_space_constraint(a, pltpu.VMEM) for a in arrays]


def in_hbm(*arrays):
    return [pltpu.with_memory_space_constraint(a, pltpu.HBM) for a in arrays]


def join_body(*refs):
    out_ref = refs[-1]
    at = 0
    for ref in refs[:-1]:
        out_ref[at : at + ref.shape[0], :] = ref[...]
        at += ref.shape[0]


def join(parts):
    rows = sum(p.shape[0] for p in parts)
    return pl.pallas_call(
        join_body, out_shape=pltpu.VMEM((rows, parts[0].shape[1]), parts[0].dtype), compiler_params=SMALL, name="join"
    )(*in_vmem(*parts))


def load_body(from_ref, out_ref, sem, *, first):
    rows = out_ref.shape[0]
    copy = pltpu.make_async_copy(from_ref.at[pl.ds(first, rows)], out_ref, sem)
    copy.start()
    copy.wait()


def load(slab, first, rows):
    return pl.pallas_call(
        functools.partial(load_body, first=first),
        in_specs=[pl.BlockSpec(memory_space=pltpu.HBM)],
        out_shape=pltpu.VMEM((rows, slab.shape[1]), slab.dtype),
        scratch_shapes=[pltpu.SemaphoreType.DMA],
        compiler_params=SMALL,
        cost_estimate=pl.CostEstimate(
            flops=0, transcendentals=0, bytes_accessed=2 * rows * slab.shape[1]
        ),
        name="load",
    )(*in_hbm(slab))


def pack_body(q_hbm, owner_hbm, row_hbm, out_ref, owner_ref, row_ref, sems, *, width, lanes, owners):
    copies = [
        pltpu.make_async_copy(owner_hbm, owner_ref, sems.at[0]),
        pltpu.make_async_copy(row_hbm, row_ref, sems.at[1]),
        pltpu.make_async_copy(q_hbm, out_ref.at[:, pl.ds(0, width)], sems.at[2]),
    ]
    for copy in copies:
        copy.start()
    copies[0].wait()
    copies[1].wait()
    lane = lax.broadcasted_iota(jnp.int32, (owner_ref.shape[0], lanes), 1)
    table = jnp.zeros(lane.shape, jnp.int32)
    for k in range(owner_ref.shape[1]):
        own = owner_ref[:, k : k + 1]
        row = row_ref[:, k : k + 1] + 1
        table += jnp.where(lane == own, row // RADIX, 0)
        table += jnp.where(lane == own + owners, row % RADIX, 0)
    out_ref[:, width:] = table.astype(jnp.float32).astype(jnp.bfloat16)
    copies[2].wait()


def score_body(x_ref, y_ref, rows_a, rows_b, rows_c, keep_ref, send_ref, g_ref, logit_ref, *, width, owners, chunk):
    rows = [
        (ref, slice(at, at + chunk))
        for ref in (rows_a, rows_b, rows_c)
        for at in range(0, ref.shape[0], chunk)
    ]
    n_q = g_ref.shape[0]
    half = n_q // 2
    g_ref[:half, :] = x_ref[...]
    g_ref[half:, :] = y_ref[...]
    n_chunks = len(rows)
    scale = PREFIX ** (-0.5)

    me = lax.axis_index("index") * lax.axis_size("query") + lax.axis_index("query")
    tab = g_ref[:, width:].astype(jnp.float32)
    lane = lax.broadcasted_iota(jnp.int32, tab.shape, 1)
    weight = jnp.where(lane == me, float(RADIX), 0.0) + jnp.where(lane == me + owners, 1.0, 0.0)
    want = jnp.sum(tab * weight, axis=1, keepdims=True).astype(jnp.int32) - 1

    best = jnp.full((n_q, 128), -jnp.inf, jnp.float32)
    score = jnp.zeros((n_q, 128), jnp.float32)
    contract = (((1,), (1,)), ((), ()))
    for c in range(n_chunks):
        at = slice(c * chunk, (c + 1) * chunk)
        ref, own = rows[c]
        logits = lax.dot_general(
            g_ref[:, :PREFIX], ref[own, :PREFIX], contract, preferred_element_type=jnp.float32
        )
        logit_ref[:, at] = logits
        for s in range(chunk // 128):
            best = jnp.maximum(best, logits[:, s * 128 : (s + 1) * 128])
    top = jnp.max(best, axis=1, keepdims=True)
    acc = jnp.zeros((n_q, PREFIX), jnp.float32)
    total = jnp.zeros((n_q, 128), jnp.float32)
    col = lax.broadcasted_iota(jnp.int32, (n_q, 128), 1)
    for c in range(n_chunks):
        at = slice(c * chunk, (c + 1) * chunk)
        ref, own = rows[c]
        full = lax.dot_general(
            g_ref[:, PREFIX:width], ref[own, PREFIX:], contract, preferred_element_type=jnp.float32
        )
        full = full + logit_ref[:, at]
        for s in range(chunk // 128):
            part = full[:, s * 128 : (s + 1) * 128]
            score += jnp.where(col + (c * chunk + s * 128) == want, part, 0.0)
        weights = jnp.exp((logit_ref[:, at] - top) * scale)
        for s in range(chunk // 128):
            total += weights[:, s * 128 : (s + 1) * 128]
        acc += jnp.dot(
            weights.astype(jnp.bfloat16), ref[own, :PREFIX], preferred_element_type=jnp.float32
        )
    total = jnp.sum(total, axis=1, keepdims=True)
    score = jnp.sum(score, axis=1, keepdims=True) * width ** (-0.5)
    tail = keep_ref.shape[1] - PREFIX
    lane = lax.broadcasted_iota(jnp.int32, (n_q, tail), 1)
    rest = jnp.where(
        lane == tail - 1, top * scale, jnp.where(lane == tail - 2, total, jnp.where(lane == me, score, 0.0))
    )
    keep_ref[:, :PREFIX] = acc[:half, :]
    keep_ref[:, PREFIX:] = rest[:half, :]
    send_ref[:, :PREFIX] = acc[half:, :]
    send_ref[:, PREFIX:] = rest[half:, :]


def merge(parts):
    wide = parts[0].shape[1]
    tops = [p[:, wide - 1 :] for p in parts]
    top = functools.reduce(jnp.maximum, tops)
    lane = lax.broadcasted_iota(jnp.int32, parts[0].shape, 1)
    scaled = (lane < PREFIX) | (lane == wide - 2)
    out = jnp.zeros(parts[0].shape, jnp.float32)
    for part, t in zip(parts, tops):
        out += part * jnp.where(scaled, jnp.exp(t - top), 1.0)
    return jnp.where(lane == wide - 1, top, out)


def merge_body(*refs, n_parts):
    out = merge([r[...] for r in refs[:n_parts]])
    at = 0
    for ref in refs[n_parts:]:
        ref[...] = out[at : at + ref.shape[0], :]
        at += ref.shape[0]


def finish_body(owner_ref, *refs, owners):
    parts, (pooled_ref, lse_ref, margin_ref) = refs[:-3], refs[-3:]
    out = merge([r[...] for r in parts])
    wide = out.shape[1]
    total = out[:, wide - 2 : wide - 1]
    lse = out[:, wide - 1 :] + jnp.log(total)
    pooled_ref[...] = out[:, :PREFIX] / total
    n = lse.shape[0]
    square = (n, n)
    eye = lax.broadcasted_iota(jnp.int32, square, 0) == lax.broadcasted_iota(jnp.int32, square, 1)
    lse_ref[...] = jnp.sum(jnp.where(eye, lse, 0.0), axis=0, keepdims=True)
    own = owner_ref[...]
    full = jnp.zeros(own.shape, jnp.float32)
    for o in range(owners):
        full += jnp.where(own == o, out[:, PREFIX + o : PREFIX + o + 1], 0.0)
    margin_ref[...] = full - lse


def on_device(queries, slab, cand_owner, cand_row, *, index_size, query_size):
    devices = index_size * query_size
    q_dev, width = queries.shape
    owners = devices
    stages = xor_stages(index_size, query_size)
    lanes = -(-2 * owners // 128) * 128
    tail = -(-(owners + 2) // 128) * 128
    f32 = jnp.float32

    x = pl.pallas_call(
        functools.partial(pack_body, width=width, lanes=lanes, owners=owners),
        in_specs=[pl.BlockSpec(memory_space=pltpu.HBM)] * 3,
        out_shape=pltpu.VMEM((q_dev, width + lanes), jnp.bfloat16),
        scratch_shapes=[
            pltpu.VMEM(cand_owner.shape, jnp.int32),
            pltpu.VMEM(cand_row.shape, jnp.int32),
            pltpu.SemaphoreType.DMA((3,)),
        ],
        compiler_params=SMALL,
        name="pack",
    )(*in_hbm(queries, cand_owner, cand_row))
    r_dev = slab.shape[0]
    chunk = r_dev // 16
    cuts = [0, 4 * chunk, 14 * chunk, r_dev]
    pieces = []
    for offs in stages[:-1]:
        got = swaps([x] * len(offs), offs, devices)
        if len(pieces) < 2:
            at = len(pieces)
            pieces.append(load(slab, cuts[at], cuts[at + 1] - cuts[at]))
        x = join([x] + got)
    y = swap(x, stages[-1][0], devices)
    pieces.append(load(slab, cuts[2], cuts[3] - cuts[2]))

    n_half = x.shape[0]
    half = min(n_half, 128)
    wide = PREFIX + tail
    pair = [pl.BlockSpec((half, width + lanes), lambda i: (i, 0))] * 2
    if n_half == half:
        pair = [pl.BlockSpec(memory_space=pltpu.VMEM)] * 2
        x, y = in_vmem(x, y)
        outs = [pl.BlockSpec(memory_space=pltpu.VMEM)] * 2
        shape = pltpu.VMEM((n_half, wide), f32)
    else:
        outs = [pl.BlockSpec((half, wide), lambda i: (i, 0))] * 2
        shape = jax.ShapeDtypeStruct((n_half, wide), f32)
    keep, send = pl.pallas_call(
        functools.partial(score_body, width=width, owners=owners, chunk=chunk),
        grid=(n_half // half,),
        in_specs=[*pair, *[pl.BlockSpec(memory_space=pltpu.VMEM)] * 3],
        out_specs=outs,
        out_shape=(shape, shape),
        scratch_shapes=[
            pltpu.VMEM((2 * half, width + lanes), jnp.bfloat16),
            pltpu.VMEM((2 * half, r_dev), f32),
        ],
        compiler_params=pltpu.CompilerParams(vmem_limit_bytes=20 << 20),
        name="score",
    )(x, y, *in_vmem(*pieces))

    parts = [keep, swap(send, stages[-1][0], devices)]
    for offs in reversed(stages[:-1]):
        n = parts[0].shape[0] // (len(offs) + 1)
        keep, *sends = pl.pallas_call(
            functools.partial(merge_body, n_parts=len(parts)),
            out_shape=tuple(pltpu.VMEM((n, wide), f32) for _ in range(len(offs) + 1)),
            compiler_params=SMALL,
            name="merge",
        )(*in_vmem(*parts))
        parts = [keep] + swaps(sends, offs, devices)
    pooled, lse, margin = pl.pallas_call(
        functools.partial(finish_body, owners=owners),
        out_shape=(
            jax.ShapeDtypeStruct((q_dev, PREFIX), f32),
            jax.ShapeDtypeStruct((1, q_dev), f32),
            jax.ShapeDtypeStruct(cand_owner.shape, f32),
        ),
        compiler_params=SMALL,
        name="finish",
    )(cand_owner, *in_vmem(*parts))
    return pooled, lse.reshape(q_dev), margin


def solution(mesh):
    spec = P(AXES, None)
    body = functools.partial(
        on_device, index_size=mesh.shape["index"], query_size=mesh.shape["query"]
    )
    return jax.shard_map(
        body,
        mesh=mesh,
        in_specs=(spec, spec, spec, spec),
        out_specs=(spec, P(AXES), spec),
        check_vma=False,
    )
```

```python
import functools
import jax
import jax.numpy as jnp
from jax import lax
from jax.experimental import pallas as pl
from jax.experimental.pallas import tpu as pltpu
from jax.sharding import PartitionSpec as P


PREFIX = 256
AXES = ("index", "query")
RADIX = 64
LOG2E = 1.4426950408889634


def xor_stages(index_size, query_size):
    q_bits = query_size.bit_length() - 1
    i_bits = index_size.bit_length() - 1
    bits = [list(range(q_bits)), list(range(q_bits + 1, q_bits + i_bits)), [q_bits]]
    stages = []
    for group in bits:
        for at in range(0, len(group), 2):
            pair = group[at : at + 2]
            offs = [1 << pair[0]]
            if len(pair) == 2:
                offs += [1 << pair[1], (1 << pair[0]) | (1 << pair[1])]
            stages.append(offs)
    return stages


def swap(x, off, devices):
    return lax.ppermute(x, AXES, [(d, d ^ off) for d in range(devices)])


SMALL = pltpu.CompilerParams(vmem_limit_bytes=16 << 20)


def swaps(arrays, offs, devices):
    out = []
    for x, off in zip(arrays, offs):
        out.append(swap(x, off, devices))
    return out


def in_vmem(*arrays):
    return [pltpu.with_memory_space_constraint(a, pltpu.VMEM) for a in arrays]


def in_hbm(*arrays):
    return [pltpu.with_memory_space_constraint(a, pltpu.HBM) for a in arrays]


def join_body(*refs):
    out_ref = refs[-1]
    at = 0
    for ref in refs[:-1]:
        out_ref[at : at + ref.shape[0], :] = ref[...]
        at += ref.shape[0]


def join(parts):
    rows = sum(p.shape[0] for p in parts)
    return pl.pallas_call(
        join_body, out_shape=pltpu.VMEM((rows, parts[0].shape[1]), parts[0].dtype), compiler_params=SMALL, name="join"
    )(*in_vmem(*parts))


def load_body(from_ref, out_ref, sem, *, first):
    rows = out_ref.shape[0]
    copy = pltpu.make_async_copy(from_ref.at[pl.ds(first, rows)], out_ref, sem)
    copy.start()
    copy.wait()


def load(slab, first, rows):
    return pl.pallas_call(
        functools.partial(load_body, first=first),
        in_specs=[pl.BlockSpec(memory_space=pltpu.HBM)],
        out_shape=pltpu.VMEM((rows, slab.shape[1]), slab.dtype),
        scratch_shapes=[pltpu.SemaphoreType.DMA],
        compiler_params=SMALL,
        cost_estimate=pl.CostEstimate(
            flops=0, transcendentals=0, bytes_accessed=2 * rows * slab.shape[1]
        ),
        name="load",
    )(*in_hbm(slab))


def pack_body(q_hbm, owner_hbm, row_hbm, out_ref, owner_ref, row_ref, sems, *, width, lanes, owners):
    copies = [
        pltpu.make_async_copy(owner_hbm, owner_ref, sems.at[0]),
        pltpu.make_async_copy(row_hbm, row_ref, sems.at[1]),
        pltpu.make_async_copy(q_hbm, out_ref.at[:, pl.ds(0, width)], sems.at[2]),
    ]
    for copy in copies:
        copy.start()
    copies[0].wait()
    copies[1].wait()
    lane = lax.broadcasted_iota(jnp.int32, (owner_ref.shape[0], lanes), 1)
    slot = jnp.where(lane < owners, lane, lane - owners)
    table = jnp.zeros(lane.shape, jnp.int32)
    own, row = owner_ref[...], row_ref[...] + 1
    for k in range(own.shape[1]):
        table = jnp.where(slot == own[:, k : k + 1], row[:, k : k + 1], table)
    table = jnp.where(lane < owners, table // RADIX, table % RADIX)
    out_ref[:, width:] = table.astype(jnp.float32).astype(jnp.bfloat16)
    copies[2].wait()


def score_body(x_ref, y_ref, rows_a, rows_b, rows_c, keep_ref, send_ref, g_ref, logit_ref, *, width, owners, chunk):
    rows = [
        (ref, slice(at, at + chunk))
        for ref in (rows_a, rows_b, rows_c)
        for at in range(0, ref.shape[0], chunk)
    ]
    n_q = g_ref.shape[0]
    half = n_q // 2
    g_ref[:half, :] = x_ref[...]
    g_ref[half:, :] = y_ref[...]
    n_chunks = len(rows)
    scale = PREFIX ** (-0.5)

    me = lax.axis_index("index") * lax.axis_size("query") + lax.axis_index("query")
    tab = g_ref[:, width:].astype(jnp.float32)
    lane = lax.broadcasted_iota(jnp.int32, tab.shape, 1)
    weight = jnp.where(lane == me, float(RADIX), 0.0) + jnp.where(lane == me + owners, 1.0, 0.0)
    want = jnp.sum(tab * weight, axis=1, keepdims=True).astype(jnp.int32) - 1

    best = jnp.full((n_q, 128), -jnp.inf, jnp.float32)
    score = jnp.zeros((n_q, 128), jnp.float32)
    contract = (((1,), (1,)), ((), ()))
    for c in range(n_chunks):
        at = slice(c * chunk, (c + 1) * chunk)
        ref, own = rows[c]
        logits = lax.dot_general(
            g_ref[:, :PREFIX], ref[own, :PREFIX], contract, preferred_element_type=jnp.float32
        )
        logit_ref[:, at] = logits
        for s in range(chunk // 128):
            best = jnp.maximum(best, logits[:, s * 128 : (s + 1) * 128])

    def rest_of(c):
        ref, own = rows[c]
        return lax.dot_general(
            g_ref[:, PREFIX:width], ref[own, PREFIX:], contract, preferred_element_type=jnp.float32
        )

    ahead = rest_of(0)
    top = jnp.max(best, axis=1, keepdims=True)
    acc = jnp.zeros((n_q, PREFIX), jnp.float32)
    total = jnp.zeros((n_q, 128), jnp.float32)
    col = lax.broadcasted_iota(jnp.int32, (n_q, 128), 1)
    for c in range(n_chunks):
        at = slice(c * chunk, (c + 1) * chunk)
        ref, own = rows[c]
        full, ahead = ahead, rest_of(c + 1) if c + 1 < n_chunks else None
        logits = logit_ref[:, at]
        full = full + logits
        for s in range(chunk // 128):
            part = full[:, s * 128 : (s + 1) * 128]
            score += jnp.where(col + (c * chunk + s * 128) == want, part, 0.0)
        weights = jnp.exp2((logits - top) * (scale * LOG2E))
        for s in range(chunk // 128):
            total += weights[:, s * 128 : (s + 1) * 128]
        acc += jnp.dot(
            weights.astype(jnp.bfloat16), ref[own, :PREFIX], preferred_element_type=jnp.float32
        )
    total = jnp.sum(total, axis=1, keepdims=True)
    score = jnp.sum(score, axis=1, keepdims=True) * width ** (-0.5)
    tail = keep_ref.shape[1] - PREFIX
    lane = lax.broadcasted_iota(jnp.int32, (n_q, tail), 1)
    rest = jnp.where(
        lane == tail - 1, top * scale, jnp.where(lane == tail - 2, total, jnp.where(lane == me, score, 0.0))
    )
    keep_ref[:, :PREFIX] = acc[:half, :]
    keep_ref[:, PREFIX:] = rest[:half, :]
    send_ref[:, :PREFIX] = acc[half:, :]
    send_ref[:, PREFIX:] = rest[half:, :]


def merge(parts):
    wide = parts[0].shape[1]
    tops = [p[:, wide - 1 :] for p in parts]
    top = functools.reduce(jnp.maximum, tops)
    lane = lax.broadcasted_iota(jnp.int32, parts[0].shape, 1)
    scaled = (lane < PREFIX) | (lane == wide - 2)
    out = jnp.zeros(parts[0].shape, jnp.float32)
    for part, t in zip(parts, tops):
        out += part * jnp.where(scaled, jnp.exp(t - top), 1.0)
    return jnp.where(lane == wide - 1, top, out)


def merge_body(*refs, n_parts):
    out = merge([r[...] for r in refs[:n_parts]])
    at = 0
    for ref in refs[n_parts:]:
        ref[...] = out[at : at + ref.shape[0], :]
        at += ref.shape[0]


def finish_body(owner_ref, *refs, owners):
    parts, (pooled_ref, lse_ref, margin_ref) = refs[:-3], refs[-3:]
    out = merge([r[...] for r in parts])
    wide = out.shape[1]
    total = out[:, wide - 2 : wide - 1]
    lse = out[:, wide - 1 :] + jnp.log(total)
    pooled_ref[...] = out[:, :PREFIX] / total
    n = lse.shape[0]
    square = (n, n)
    eye = lax.broadcasted_iota(jnp.int32, square, 0) == lax.broadcasted_iota(jnp.int32, square, 1)
    lse_ref[...] = jnp.sum(jnp.where(eye, lse, 0.0), axis=0, keepdims=True)
    own = owner_ref[...]
    full = jnp.zeros(own.shape, jnp.float32)
    for o in range(owners):
        full += jnp.where(own == o, out[:, PREFIX + o : PREFIX + o + 1], 0.0)
    margin_ref[...] = full - lse


def on_device(queries, slab, cand_owner, cand_row, *, index_size, query_size):
    devices = index_size * query_size
    q_dev, width = queries.shape
    owners = devices
    stages = xor_stages(index_size, query_size)
    lanes = -(-2 * owners // 128) * 128
    tail = -(-(owners + 2) // 128) * 128
    f32 = jnp.float32

    x = pl.pallas_call(
        functools.partial(pack_body, width=width, lanes=lanes, owners=owners),
        in_specs=[pl.BlockSpec(memory_space=pltpu.HBM)] * 3,
        out_shape=pltpu.VMEM((q_dev, width + lanes), jnp.bfloat16),
        scratch_shapes=[
            pltpu.VMEM(cand_owner.shape, jnp.int32),
            pltpu.VMEM(cand_row.shape, jnp.int32),
            pltpu.SemaphoreType.DMA((3,)),
        ],
        compiler_params=SMALL,
        name="pack",
    )(*in_hbm(queries, cand_owner, cand_row))
    r_dev = slab.shape[0]
    chunk = r_dev // 16
    cuts = [0, 3 * chunk, 14 * chunk, r_dev]
    pieces = []
    for offs in stages[:-1]:
        got = swaps([x] * len(offs), offs, devices)
        if len(pieces) < 2:
            at = len(pieces)
            pieces.append(load(slab, cuts[at], cuts[at + 1] - cuts[at]))
        x = join([x] + got)
    y = swap(x, stages[-1][0], devices)
    pieces.append(load(slab, cuts[2], cuts[3] - cuts[2]))

    n_half = x.shape[0]
    half = min(n_half, 128)
    wide = PREFIX + tail
    pair = [pl.BlockSpec((half, width + lanes), lambda i: (i, 0))] * 2
    if n_half == half:
        pair = [pl.BlockSpec(memory_space=pltpu.VMEM)] * 2
        x, y = in_vmem(x, y)
        outs = [pl.BlockSpec(memory_space=pltpu.VMEM)] * 2
        shape = pltpu.VMEM((n_half, wide), f32)
    else:
        outs = [pl.BlockSpec((half, wide), lambda i: (i, 0))] * 2
        shape = jax.ShapeDtypeStruct((n_half, wide), f32)
    keep, send = pl.pallas_call(
        functools.partial(score_body, width=width, owners=owners, chunk=chunk),
        grid=(n_half // half,),
        in_specs=[*pair, *[pl.BlockSpec(memory_space=pltpu.VMEM)] * 3],
        out_specs=outs,
        out_shape=(shape, shape),
        scratch_shapes=[
            pltpu.VMEM((2 * half, width + lanes), jnp.bfloat16),
            pltpu.VMEM((2 * half, r_dev), f32),
        ],
        compiler_params=pltpu.CompilerParams(vmem_limit_bytes=20 << 20),
        name="score",
    )(x, y, *in_vmem(*pieces))

    parts = [keep, swap(send, stages[-1][0], devices)]
    for offs in reversed(stages[:-1]):
        n = parts[0].shape[0] // (len(offs) + 1)
        keep, *sends = pl.pallas_call(
            functools.partial(merge_body, n_parts=len(parts)),
            out_shape=tuple(pltpu.VMEM((n, wide), f32) for _ in range(len(offs) + 1)),
            compiler_params=SMALL,
            name="merge",
        )(*in_vmem(*parts))
        parts = [keep] + swaps(sends, offs, devices)
    pooled, lse, margin = pl.pallas_call(
        functools.partial(finish_body, owners=owners),
        out_shape=(
            jax.ShapeDtypeStruct((q_dev, PREFIX), f32),
            jax.ShapeDtypeStruct((1, q_dev), f32),
            jax.ShapeDtypeStruct(cand_owner.shape, f32),
        ),
        compiler_params=SMALL,
        name="finish",
    )(cand_owner, *in_vmem(*parts))
    return pooled, lse.reshape(q_dev), margin


def solution(mesh):
    spec = P(AXES, None)
    body = functools.partial(
        on_device, index_size=mesh.shape["index"], query_size=mesh.shape["query"]
    )
    return jax.shard_map(
        body,
        mesh=mesh,
        in_specs=(spec, spec, spec, spec),
        out_specs=(spec, P(AXES), spec),
        check_vma=False,
    )
```
